256 devices in a mesh: fsdp: 32 (over z_hi, x, core), dp: 8 (over y, z_lo).
Axes of the slice: x: 4, y: 4, z: 8 (z_hi: 4, z_lo: 2; z = z_hi * 2 + z_lo), core: 2. Of those that a mesh axis runs over, the one named last changes fastest.
Arguments:
- activations: bfloat16 [65536, 4096], P(('fsdp', 'dp')), may hold values from -6 to 6
- cotangents: bfloat16 [2, 65536, 4096], P(None, ('fsdp', 'dp')), may hold values from -6 to 6
- weights: bfloat16 [2, 4096, 4096], P(None, 'fsdp'), may hold values from -4 to 4
- projectors: bfloat16 [2, 4096, 512], P(None, 'fsdp'), may hold values from -0.09375 to 0.09375
- first_moment: float32 [2, 4096, 512], P(None, 'fsdp'), may hold values from -3 to 3
- second_moment: float32 [2, 4096, 512], P(None, 'fsdp'), may hold values from 0.25 to 4
- matrix_settings: int32 [2, 2], replicated, may hold values from 0 to 512, as said below
Outputs:
- new_weights: bfloat16 [2, 4096, 4096], P(None, 'fsdp')
- new_first: float32 [2, 4096, 512], P(None, 'fsdp')
- new_second: float32 [2, 4096, 512], P(None, 'fsdp')
The draws below stay inside these ranges and needn't reach their ends.
Inputs may be any that keep to these rules, and one draw needn't show every extreme that they name: `matrix_settings`: column 0 is a rank from 128 to 512, some matrix has rank exactly 512; column 1 is 0 (the projector acts on the activations) or 1 (on the cotangents), and both values occur.
All inputs are finite; a program needn't handle non-finite values.
Results may differ from the reference program's by a relative error of at most 0.0045.
Values may be sent and summed in bfloat16 or wider, within the bound.
No kernel may reach another device: no remote copies, remote signals or barrier semaphores. Data moves between devices by JAX's collectives and lax.ppermute only.
A program may use at most 128 MiB of HBM per device.

```python
import math
import jax
import jax.numpy as jnp
from jax import lax

D = 4096
MATS = 2
RMAX = 512
TOKENS = 65536


def draw_matrix_settings(key, part):
    first_key, second_key = jax.random.split(jax.random.fold_in(key, 17))
    drawn = jax.random.randint(first_key, (MATS,), RMAX // 4, RMAX + 1)
    chosen = jax.random.randint(second_key, (), 0, MATS)
    ranks = jnp.where(jnp.arange(MATS) == chosen, RMAX, drawn)
    offset = jax.random.randint(jax.random.fold_in(key, 29), (), 0, 2)
    sides = (jnp.arange(MATS) + offset) % 2
    return jnp.stack([ranks, sides], axis=1).astype(jnp.int32)


def level_of(stream_key, dims, cuts, low, largest):
    loudness, own = 1.0, jax.random.fold_in(stream_key, 6)
    for position, blocks in cuts:
        steps = jnp.exp(jax.random.uniform(jax.random.fold_in(own, position), (blocks,), jnp.float32, low / len(cuts), largest / len(cuts)))
        loudness = loudness * jnp.repeat(steps, dims[position] // blocks).reshape([-1 if axis == position else 1 for axis in range(len(dims))])
    return loudness


def scatter_about(rng, extent, width, bound, cuts=(), held_as=jnp.bfloat16):
    values = width * jax.random.normal(rng, extent, jnp.float32)
    if cuts:
        values = values * level_of(rng, extent, cuts, -0.22, 0.18)
    return jnp.clip(values, -bound, bound).astype(held_as)


def setup_inputs(seed: int = 0) -> dict:
    key_of = jax.random.split(jax.random.key(seed), 8)
    return {
        "activations": scatter_about(key_of[0], (TOKENS, D), 1.0, 6.0, ((0, 256),)),
        "cotangents": scatter_about(key_of[1], (MATS, TOKENS, D), 1.0, 6.0, ((1, 256),)),
        "weights": scatter_about(key_of[2], (MATS, D, D), 0.5, 4.0, ((1, 32),)),
        "projectors": scatter_about(key_of[3], (MATS, D, RMAX), D ** -0.5, 0.09375, ((1, 32),)),
        "first_moment": scatter_about(key_of[4], (MATS, D, RMAX), 0.5, 3.0, ((1, 32),), jnp.float32),
        "second_moment": jnp.clip(jnp.exp(math.log(4.0) - 2.7725887 * jax.random.uniform(key_of[5], (MATS, D, RMAX), jnp.float32) ** level_of(key_of[5], (MATS, D, RMAX), ((1, 32),), -0.2, 0.2)), 0.25, 4.0),
        "matrix_settings": draw_matrix_settings(jax.random.fold_in(key_of[7], 71), 0),
    }


BETA_ONE = 0.9
BETA_TWO = 0.95
EPSILON = 1e-08

def contract_tokens(left_operand, right_operand):
    return lax.dot_general(left_operand, right_operand, (((0,), (0,)), ((), ())), preferred_element_type=jnp.float32)

def reference(activations, cotangents, weights, projectors, first_moment, second_moment, matrix_settings):
    grad_scale = 1.0 / math.sqrt(activations.shape[0])
    rank_columns = jnp.arange(projectors.shape[2])
    weight_list, first_list, second_list = ([], [], [])
    for matrix_index in range(cotangents.shape[0]):
        live_mask = (rank_columns < matrix_settings[matrix_index, 0])[None, :]
        on_inputs = matrix_settings[matrix_index, 1] == 0
        projector = jnp.where(live_mask, projectors[matrix_index], jnp.zeros((), projectors.dtype))
        grads_out = cotangents[matrix_index]
        coeffs = lax.cond(on_inputs, lambda: jnp.dot(activations, projector, preferred_element_type=jnp.float32), lambda: jnp.dot(grads_out, projector, preferred_element_type=jnp.float32)).astype(jnp.bfloat16)
        projected = lax.cond(on_inputs, lambda: contract_tokens(grads_out, coeffs), lambda: contract_tokens(activations, coeffs)) * grad_scale
        moment_one = jnp.where(live_mask, BETA_ONE * first_moment[matrix_index] + (1.0 - BETA_ONE) * projected, 0.0)
        moment_two = jnp.where(live_mask, BETA_TWO * second_moment[matrix_index] + (1.0 - BETA_TWO) * projected * projected, 0.0)
        normalized = jnp.where(live_mask, moment_one / (jnp.sqrt(moment_two) + EPSILON), 0.0).astype(jnp.bfloat16)
        update = lax.dot_general(normalized, projector, (((1,), (1,)), ((), ())), preferred_element_type=jnp.float32)
        weight_list.append((weights[matrix_index].astype(jnp.float32) - update).astype(jnp.bfloat16))
        first_list.append(moment_one)
        second_list.append(moment_two)
    return (jnp.stack(weight_list), jnp.stack(first_list), jnp.stack(second_list))
```

```python
import math

import jax
import jax.numpy as jnp
from jax import lax
from jax.sharding import Mesh, PartitionSpec as P

BETA_ONE = 0.9
BETA_TWO = 0.95
EPSILON = 1e-08
ZH, X, C, Y, ZL = SIZES = (4, 4, 2, 4, 2)
NAMES = ("zh", "x", "core", "y", "zl")
BF16 = jnp.bfloat16
F32 = jnp.float32


def flat_index(zh, x, c, y, zl):
    return (((zh * X + x) * C + c) * Y + y) * ZL + zl


def line_groups(axis_of_core):
    groups = []
    for c in range(C):
        for zh in range(ZH):
            for zl in range(ZL):
                for fixed in range(4):
                    if axis_of_core[c] == "x":
                        groups.append([flat_index(zh, i, c, fixed, zl) for i in range(X)])
                    else:
                        groups.append([flat_index(zh, fixed, c, i, zl) for i in range(Y)])
    return groups


WIDE = line_groups("xy")
NARROW = line_groups("yx")


def swap_lines(v, groups):
    return lax.all_to_all(
        v, NAMES, split_axis=0, concat_axis=0, tiled=True, axis_index_groups=groups
    )


def swap_axes(v, axes):
    return lax.all_to_all(v, axes, split_axis=0, concat_axis=0, tiled=True)


def repeat(v, n):
    return jnp.broadcast_to(v[None], (n,) + v.shape)


def to_partner(v):
    return lax.ppermute(v, "core", [(0, 1), (1, 0)])


def on_device(
    activations, cotangents, weights, projectors, first_moment, second_moment, matrix_settings
):
    mats, rows, rank_max = projectors.shape
    token_total = activations.shape[0] * 256
    grad_scale = 1.0 / math.sqrt(token_total)
    core = lax.axis_index("core")
    y = lax.axis_index("y")
    zl = lax.axis_index("zl")
    live = jnp.arange(rank_max)[None, None, :] < matrix_settings[:, 0][:, None, None]
    half, quarter = rows // ZL, rank_max // Y

    a_far = to_partner(activations)
    c_far = to_partner(lax.dynamic_index_in_dim(cotangents, 1 - core, 0, keepdims=False))
    c_near = lax.dynamic_index_in_dim(cotangents, core, 0, keepdims=False)

    masked = jnp.where(live, projectors, jnp.zeros((), BF16))
    piece = lax.dynamic_slice(masked, (0, zl * half, y * quarter), (mats, half, quarter))
    piece = jnp.broadcast_to(piece[None], (ZH * ZL, mats, half, quarter))
    g = swap_axes(piece.reshape(ZH * ZL * C, half, quarter), ("zh", "zl", "core"))
    g = swap_lines(repeat(g, 4), NARROW)
    g = swap_lines(repeat(g, 4), WIDE)
    g = g.reshape(4, 4, ZH, ZL, C, half, quarter)
    full = jnp.where(
        core == 0, g.transpose(2, 0, 4, 3, 5, 1, 6), g.transpose(2, 1, 4, 3, 5, 0, 6)
    ).reshape(ZH * X * C * rows, rank_max)

    on_inputs = lax.dynamic_index_in_dim(matrix_settings[:, 1], core, 0, keepdims=False) == 0
    partial = 0.0
    for a, b in ((activations, c_near), (a_far, c_far)):
        coeffs = jnp.dot(
            jnp.where(on_inputs, a, b), full, preferred_element_type=F32
        ).astype(BF16)
        partial = partial + lax.dot_general(
            jnp.where(on_inputs, b, a), coeffs, (((0,), (0,)), ((), ())),
            preferred_element_type=F32,
        )
    partial = partial.astype(BF16).reshape(ZH, X, C, ZL, half, Y, quarter)
    full_far = to_partner(full)
    s = jnp.where(
        core == 0,
        partial.transpose(1, 5, 0, 3, 2, 4, 6),
        partial.transpose(5, 1, 0, 3, 2, 4, 6),
    )
    s = swap_lines(s, WIDE)
    s = jnp.sum(s.astype(F32), axis=0).astype(BF16)
    s = swap_lines(s, NARROW)
    s = jnp.sum(s.astype(F32), axis=0).astype(BF16)
    s = swap_axes(s.reshape(ZH * ZL * C, half, quarter), ("zh", "zl", "core"))
    s = jnp.sum(s.astype(F32).reshape(ZH * ZL, mats, half, quarter), axis=0).astype(BF16)
    s = swap_axes(repeat(s, Y * ZL), ("y", "zl"))
    s = s.reshape(Y, ZL, mats, half, quarter).transpose(2, 1, 3, 0, 4)
    projected = s.reshape(mats, rows, rank_max).astype(F32) * grad_scale

    moment_one = jnp.where(live, BETA_ONE * first_moment + (1.0 - BETA_ONE) * projected, 0.0)
    moment_two = jnp.where(
        live, BETA_TWO * second_moment + (1.0 - BETA_TWO) * projected * projected, 0.0
    )
    normalized = jnp.where(
        live, moment_one / (jnp.sqrt(moment_two) + EPSILON), 0.0
    ).astype(BF16)
    updates = []
    for k, proj in ((core, full), (1 - core, full_far)):
        n = lax.dynamic_index_in_dim(normalized, k, 0, keepdims=False)
        updates.append(
            lax.dot_general(n, proj, (((1,), (1,)), ((), ())), preferred_element_type=F32)
        )
    near, far = updates
    update = jnp.where(core == 0, jnp.stack([near, far]), jnp.stack([far, near]))
    return ((weights.astype(F32) - update).astype(BF16), moment_one, moment_two)


def solution(mesh):
    split = Mesh(mesh.devices.reshape(SIZES), NAMES)
    owner = ("zh", "x", "core")
    return jax.shard_map(
        on_device,
        mesh=split,
        in_specs=(
            P(NAMES, None),
            P(None, NAMES, None),
            P(None, owner, None),
            P(None, owner, None),
            P(None, owner, None),
            P(None, owner, None),
            P(),
        ),
        out_specs=(P(None, owner, None), P(None, owner, None), P(None, owner, None)),
        check_vma=False,
    )
```

```python
import functools
import math

import jax
import jax.numpy as jnp
from jax import lax
from jax.experimental import pallas as pl
from jax.experimental.pallas import tpu as pltpu
from jax.sharding import Mesh, PartitionSpec as P


BETA_ONE = 0.9
BETA_TWO = 0.95
EPSILON = 1e-08
ZH, X, C, Y, ZL = SIZES = (4, 4, 2, 4, 2)
NAMES = ("zh", "x", "core", "y", "zl")
BF16 = jnp.bfloat16
F32 = jnp.float32
VMEM = pltpu.MemorySpace.VMEM
SMEM = pltpu.MemorySpace.SMEM
PARAMS = pltpu.CompilerParams(vmem_limit_bytes=28 << 20)


def flat_index(zh, x, c, y, zl):
    return (((zh * X + x) * C + c) * Y + y) * ZL + zl


def line_groups(axis_of_core):
    groups = []
    for c in range(C):
        for zh in range(ZH):
            for zl in range(ZL):
                for fixed in range(4):
                    if axis_of_core[c] == "x":
                        groups.append([flat_index(zh, i, c, fixed, zl) for i in range(X)])
                    else:
                        groups.append([flat_index(zh, fixed, c, i, zl) for i in range(Y)])
    return groups


WIDE = line_groups("xy")
NARROW = line_groups("yx")


def shift(v, groups, offset):
    pairs = [(g[i], g[(i + offset) % 4]) for g in groups for i in range(4)]
    return lax.ppermute(v, NAMES, pairs)


def swap_lines(v, groups):
    return lax.all_to_all(
        v, NAMES, split_axis=0, concat_axis=0, tiled=True, axis_index_groups=groups
    )


def swap_axes(v, axes):
    return lax.all_to_all(v, axes, split_axis=0, concat_axis=0, tiled=True)


def repeat(v, n):
    return jnp.broadcast_to(v[None], (n,) + v.shape)


def to_partner(v):
    return lax.ppermute(v, "core", [(0, 1), (1, 0)])


def place(core, a, b):
    first = core == 0
    return jnp.where(first, a, b), jnp.where(first, b, a)


def coeffs_kernel(count, first, last, pos, x_ref, *refs):
    blocks, refs = refs[:count], refs[count:]
    acc = refs[-1]
    if first:
        acc[...] = jnp.zeros_like(acc)
    else:
        acc[...] = refs[0][...]
    for i in range(count):
        for b in range(4):
            x, y = place(pos[0], pos[1 + i], b)
            lhs = jnp.concatenate(
                [
                    x_ref[:, pl.ds(pl.multiple_of((zh * X + x) * 256, 256), 256)]
                    for zh in range(ZH)
                ],
                axis=1,
            )
            rhs = blocks[i][b].reshape(ZH * 256, 128)
            acc[y] += jnp.dot(lhs, rhs, preferred_element_type=F32)
    if last:
        refs[-2][...] = acc[...].astype(BF16)


def coeffs_step(pos, x, blocks, acc=None, last=False):
    tokens = x.shape[0]
    shape = (4, tokens, 128)
    ins = [pos, x, *blocks] + ([] if acc is None else [acc])
    return pl.pallas_call(
        functools.partial(coeffs_kernel, len(blocks), acc is None, last),
        out_shape=jax.ShapeDtypeStruct(shape, BF16 if last else F32),
        in_specs=[pl.BlockSpec(memory_space=SMEM)]
        + [pl.BlockSpec(memory_space=VMEM)] * (len(ins) - 1),
        out_specs=pl.BlockSpec(memory_space=VMEM),
        scratch_shapes=[pltpu.VMEM(shape, F32)] if last else [],
        compiler_params=PARAMS,
        name="coeffs",
    )(*ins)


def grad_kernel(pos, xt_ref, coeffs_ref, out_ref):
    for b in range(4):
        x, y = place(pos[0], pos[1], b)
        lhs = jnp.concatenate([xt_ref[zh, x] for zh in range(ZH)], axis=0)
        part = jnp.dot(lhs, coeffs_ref[y], preferred_element_type=F32)
        out_ref[b] = part.astype(BF16).reshape(ZH, 256, 128)


def grad_block(pos, xt, coeffs):
    return pl.pallas_call(
        grad_kernel,
        out_shape=jax.ShapeDtypeStruct((4, ZH, 256, 128), BF16),
        in_specs=[pl.BlockSpec(memory_space=SMEM)] + [pl.BlockSpec(memory_space=VMEM)] * 2,
        out_specs=pl.BlockSpec(memory_space=VMEM),
        compiler_params=PARAMS,
        name="grads",
    )(pos, xt, coeffs)


def order_kernel(pos, *refs):
    out_ref = refs[4]
    for i in range(4):
        for b in range(4):
            x, y = place(pos[0], pos[1 + i], b)
            for zh in range(ZH):
                lanes = pl.ds(pl.multiple_of((zh * X + x) * 256, 256), 256)
                out_ref[y, :, lanes] = refs[i][b, zh].T


def in_order(pos, blocks):
    return pl.pallas_call(
        order_kernel,
        out_shape=jax.ShapeDtypeStruct((Y, 128, ZH * X * 256), BF16),
        in_specs=[pl.BlockSpec(memory_space=SMEM)] + [pl.BlockSpec(memory_space=VMEM)] * 4,
        out_specs=pl.BlockSpec(memory_space=VMEM),
        compiler_params=PARAMS,
        name="order",
    )(pos, *blocks)


def sides_kernel(pos, a_near, a_far, c_near, c_far, x_ref, xt_ref):
    tokens = a_near.shape[0]

    def write(projected, other):
        x_ref[:tokens, :] = projected[0]
        x_ref[tokens:, :] = projected[1]
        xt_ref[:, :tokens] = other[0].T
        xt_ref[:, tokens:] = other[1].T

    a = lambda: (a_near[...], a_far[...])
    c = lambda: (c_near[0], c_far[...])

    @pl.when(pos[1] == 0)
    def _():
        write(a(), c())

    @pl.when(pos[1] != 0)
    def _():
        write(c(), a())


def make_sides(pos, a_near, a_far, cotangents, c_far):
    tokens, features = a_near.shape
    chunk = 512
    block = pl.BlockSpec((tokens, chunk), lambda j, pos: (0, j))
    return pl.pallas_call(
        sides_kernel,
        out_shape=(
            jax.ShapeDtypeStruct((2 * tokens, features), BF16),
            jax.ShapeDtypeStruct((features, 2 * tokens), BF16),
        ),
        grid_spec=pltpu.PrefetchScalarGridSpec(
            num_scalar_prefetch=1,
            grid=(features // chunk,),
            in_specs=[
                block,
                block,
                pl.BlockSpec((1, tokens, chunk), lambda j, pos: (pos[0], 0, j)),
                block,
            ],
            out_specs=(
                pl.BlockSpec((2 * tokens, chunk), lambda j, pos: (0, j)),
                pl.BlockSpec((chunk, 2 * tokens), lambda j, pos: (j, 0)),
            ),
        ),
        compiler_params=PARAMS,
        name="sides",
    )(pos, a_near, a_far, cotangents, c_far)


def update_kernel(
    scale, pos, settings, s_ref, m1_ref, m2_ref, near_ref, far_ref, w_ref,
    w_out, m1_out, m2_out, n_ref,
):
    mats = m1_ref.shape[0]
    half, quarter = s_ref.shape[3:]
    for k in range(mats):
        for y in range(Y):
            columns = slice(y * quarter, (y + 1) * quarter)
            column = lax.broadcasted_iota(jnp.int32, (half, quarter), 1) + y * quarter
            live = column < settings[k, 0]
            for z in range(ZL):
                rows = slice(z * half, (z + 1) * half)
                grad = s_ref[y, z, k].astype(F32) * scale
                m1 = BETA_ONE * m1_ref[k, rows, columns] + (1.0 - BETA_ONE) * grad
                m2 = BETA_TWO * m2_ref[k, rows, columns] + (1.0 - BETA_TWO) * grad * grad
                m1 = jnp.where(live, m1, 0.0)
                m2 = jnp.where(live, m2, 0.0)
                m1_out[k, rows, columns] = m1
                m2_out[k, rows, columns] = m2
                normalized = jnp.where(live, m1 / (jnp.sqrt(m2) + EPSILON), 0.0)
                n_ref[k, rows, columns] = normalized.astype(BF16)
    for k, p_ref in ((pos[0], near_ref), (1 - pos[0], far_ref)):
        n = n_ref[k]
        for j in range(0, w_ref.shape[2], 512):
            lanes = slice(j, j + 512)
            rhs = p_ref[:, :, lanes].reshape(Y * quarter, 512)
            update = jnp.dot(n, rhs, preferred_element_type=F32)
            w_out[k, :, lanes] = (w_ref[k, :, lanes].astype(F32) - update).astype(BF16)


def apply_update(scale, pos, settings, s, m1, m2, near, far, weights):
    return pl.pallas_call(
        functools.partial(update_kernel, scale),
        out_shape=(
            jax.ShapeDtypeStruct(weights.shape, BF16),
            jax.ShapeDtypeStruct(m1.shape, F32),
            jax.ShapeDtypeStruct(m2.shape, F32),
        ),
        in_specs=[pl.BlockSpec(memory_space=SMEM)] * 2
        + [pl.BlockSpec(memory_space=VMEM)] * 6,
        out_specs=(pl.BlockSpec(memory_space=VMEM),) * 3,
        scratch_shapes=[pltpu.VMEM(m1.shape, BF16)],
        compiler_params=PARAMS,
        name="update",
    )(pos, settings, s, m1, m2, near, far, weights)


def on_device(
    activations, cotangents, weights, projectors, first_moment, second_moment, matrix_settings
):
    mats, rows, rank_max = projectors.shape
    token_total = activations.shape[0] * 256
    grad_scale = 1.0 / math.sqrt(token_total)
    core = lax.axis_index("core")
    y = lax.axis_index("y")
    zl = lax.axis_index("zl")
    mine = jnp.where(core == 0, lax.axis_index("x"), y)
    live = jnp.arange(rank_max)[None, None, :] < matrix_settings[:, 0][:, None, None]
    half, quarter = rows // ZL, rank_max // Y

    def positions(*offsets):
        return jnp.stack([core] + [(mine + o) % 4 for o in offsets]).astype(jnp.int32)

    far_index = 1 - core
    a_far = to_partner(activations)
    c_far = to_partner(lax.dynamic_index_in_dim(cotangents, far_index, 0, keepdims=False))

    masked = jnp.where(live, projectors, jnp.zeros((), BF16))
    piece = lax.dynamic_slice(masked, (0, zl * half, y * quarter), (mats, half, quarter))
    piece = jnp.broadcast_to(piece[None, :, None], (ZH, mats, ZL, half, quarter))
    g = swap_axes(piece.reshape(ZH * C * ZL, half, quarter), ("zh", "core", "zl"))
    g = swap_lines(repeat(g.reshape(ZH, 256, quarter), 4), NARROW)
    g = g.reshape(4, ZH, 256, quarter)
    by_offset = {0: g}
    for o in (1, 3, 2):
        by_offset[o] = shift(g, WIDE, o)

    side = lax.dynamic_index_in_dim(matrix_settings[:, 1], core, 0, keepdims=False)
    projected_side, other_side = make_sides(
        jnp.stack([core, side]).astype(jnp.int32), activations, a_far, cotangents, c_far
    )
    other_side = other_side.reshape(ZH, X, 256, 512)

    acc = coeffs_step(positions(0), projected_side, [g])
    acc = coeffs_step(positions(-1, -3), projected_side, [by_offset[1], by_offset[3]], acc)
    coeffs = coeffs_step(positions(-2), projected_side, [by_offset[2]], acc, last=True)

    parts = []
    for o in (2, 1, 3):
        block = grad_block(positions(o), other_side, coeffs)
        parts.append(shift(block, WIDE, o))
    s = grad_block(positions(0), other_side, coeffs)
    full = in_order(positions(0, -1, -2, -3), [by_offset[o] for o in range(4)])
    full_far = to_partner(full)
    s = s.astype(F32)
    for part in parts:
        s = s + part.astype(F32)

    s = swap_lines(s.astype(BF16), NARROW).reshape(4, ZH, 256, quarter)
    s = jnp.sum(s.astype(F32), axis=0).astype(BF16)
    s = swap_axes(s.reshape(ZH * C * ZL, half, quarter), ("zh", "core", "zl"))
    s = s.astype(F32).reshape(ZH, mats, ZL, half, quarter)
    s = jnp.sum(s, axis=(0, 2)).astype(BF16)
    s = swap_axes(repeat(s, Y * ZL), ("y", "zl"))
    return apply_update(
        grad_scale,
        positions(),
        matrix_settings,
        s.reshape(Y, ZL, mats, half, quarter),
        first_moment,
        second_moment,
        full,
        full_far,
        weights,
    )


def solution(mesh):
    split = Mesh(mesh.devices.reshape(SIZES), NAMES)
    owner = ("zh", "x", "core")
    return jax.shard_map(
        on_device,
        mesh=split,
        in_specs=(
            P(NAMES, None),
            P(None, NAMES, None),
            P(None, owner, None),
            P(None, owner, None),
            P(None, owner, None),
            P(None, owner, None),
            P(),
        ),
        out_specs=(P(None, owner, None), P(None, owner, None), P(None, owner, None)),
        check_vma=False,
    )
```

```python
import functools
import math

import jax
import jax.numpy as jnp
from jax import lax
from jax.experimental import pallas as pl
from jax.experimental.pallas import tpu as pltpu
from jax.sharding import Mesh, PartitionSpec as P


BETA_ONE = 0.9
BETA_TWO = 0.95
EPSILON = 1e-08
ZH, X, C, Y, ZL = SIZES = (4, 4, 2, 4, 2)
NAMES = ("zh", "x", "core", "y", "zl")
BF16 = jnp.bfloat16
F32 = jnp.float32
VMEM = pltpu.MemorySpace.VMEM
SMEM = pltpu.MemorySpace.SMEM
HBM = pltpu.MemorySpace.HBM


def mib(count):
    return pltpu.CompilerParams(vmem_limit_bytes=count << 20)


def flat_index(zh, x, c, y, zl):
    return (((zh * X + x) * C + c) * Y + y) * ZL + zl


def line_groups(axis_of_core):
    groups = []
    for c in range(C):
        for zh in range(ZH):
            for zl in range(ZL):
                for fixed in range(4):
                    if axis_of_core[c] == "x":
                        groups.append([flat_index(zh, i, c, fixed, zl) for i in range(X)])
                    else:
                        groups.append([flat_index(zh, fixed, c, i, zl) for i in range(Y)])
    return groups


WIDE = line_groups("xy")
NARROW = line_groups("yx")


def shift(v, groups, offset):
    pairs = [(g[i], g[(i + offset) % 4]) for g in groups for i in range(4)]
    return lax.ppermute(v, NAMES, pairs)


def swap_axes(v, axes):
    return lax.all_to_all(v, axes, split_axis=0, concat_axis=0, tiled=True)


def repeat(v, n):
    return jnp.broadcast_to(v[None], (n,) + v.shape)


def to_partner(v):
    return lax.ppermute(v, "core", [(0, 1), (1, 0)])


def place(core, a, b):
    first = core == 0
    return jnp.where(first, a, b), jnp.where(first, b, a)


def offset(position, shift_by):
    return (position + shift_by) & 3


def views(block, zh_from):
    if len(block.shape) == 4:
        return [(block, zh_from)]
    return [(block.at[h], zh_from + h * block.shape[2]) for h in range(block.shape[0])]


def coeffs_kernel(items, first, last, pos, x_ref, *refs):
    blocks, refs = refs[: len(items)], refs[len(items) :]
    acc = refs[-1]
    if first:
        acc[...] = jnp.zeros_like(acc)
    else:
        acc[...] = refs[0][...]
    for (a_off, b_offs, start), whole_block in zip(items, blocks):
        for i, b_off, (block, zh_from) in [
            (i, b_off, view)
            for view in views(whole_block, start)
            for i, b_off in enumerate(b_offs)
        ]:
            count = block.shape[1]
            x, y = place(pos[0], offset(pos[1], a_off), offset(pos[2], b_off))
            lhs = jnp.concatenate(
                [
                    x_ref[:, pl.ds(pl.multiple_of((zh * X + x) * 256, 256), 256)]
                    for zh in range(zh_from, zh_from + count)
                ],
                axis=1,
            )
            rhs = block[i].reshape(count * 256, 128)
            acc[y] += jnp.dot(lhs, rhs, preferred_element_type=F32)
    if last:
        refs[-2][...] = acc[...].astype(BF16)


def coeffs_step(pos, x, blocks, acc=None, last=False):
    shape = (4, x.shape[0], 128)
    items = tuple(block[1:] for block in blocks)
    ins = [pos, x, *(block[0] for block in blocks)] + ([] if acc is None else [acc])
    return pl.pallas_call(
        functools.partial(coeffs_kernel, items, acc is None, last),
        out_shape=jax.ShapeDtypeStruct(shape, BF16 if last else F32),
        in_specs=[pl.BlockSpec(memory_space=SMEM)]
        + [pl.BlockSpec(memory_space=VMEM)] * (len(ins) - 1),
        out_specs=pl.BlockSpec(memory_space=VMEM),
        scratch_shapes=[pltpu.VMEM(shape, F32)] if last else [],
        compiler_params=mib(14),
        name="coeffs",
    )(*ins)


def grad_kernel(items, pos, xt_ref, coeffs_ref, *out_refs):
    for (a_off, b_offs), out_ref in zip(items, out_refs):
        for i, b_off in enumerate(b_offs):
            x, y = place(pos[0], offset(pos[1], a_off), offset(pos[2], b_off))
            lhs = jnp.concatenate([xt_ref[zh, x] for zh in range(ZH)], axis=0)
            part = jnp.dot(lhs, coeffs_ref[y], preferred_element_type=F32)
            out_ref[i] = part.astype(BF16).reshape(ZH, 256, 128)


def grad_blocks(pos, xt, coeffs, *items):
    shapes = [
        jax.ShapeDtypeStruct((len(b_offs), ZH, 256, 128), BF16) for _, b_offs in items
    ]
    return pl.pallas_call(
        functools.partial(grad_kernel, items),
        out_shape=shapes,
        in_specs=[pl.BlockSpec(memory_space=SMEM)] + [pl.BlockSpec(memory_space=VMEM)] * 2,
        out_specs=[pl.BlockSpec(memory_space=VMEM)] * len(shapes),
        compiler_params=mib(12),
        name="grads",
    )(pos, xt, coeffs)


def order_kernel(items, pos, *refs):
    out_ref = refs[-1]
    for (a_off, b_offs, start), whole_block in zip(items, refs):
        for i, b_off, (block, zh_from) in [
            (i, b_off, view)
            for view in views(whole_block, start)
            for i, b_off in enumerate(b_offs)
        ]:
            x, y = place(pos[0], offset(pos[1], a_off), offset(pos[2], b_off))
            for j in range(block.shape[1]):
                lanes = pl.ds(pl.multiple_of(((zh_from + j) * X + x) * 256, 256), 256)
                out_ref[y, :, lanes] = block[i, j].T


def in_order(pos, blocks):
    return pl.pallas_call(
        functools.partial(order_kernel, tuple(block[1:] for block in blocks)),
        out_shape=jax.ShapeDtypeStruct((Y, 128, ZH * X * 256), BF16),
        in_specs=[pl.BlockSpec(memory_space=SMEM)]
        + [pl.BlockSpec(memory_space=VMEM)] * len(blocks),
        out_specs=pl.BlockSpec(memory_space=VMEM),
        compiler_params=mib(12),
        name="order",
    )(pos, *(block[0] for block in blocks))


def piece_kernel(pos, settings, p_ref, out_ref):
    mats, half, quarter = p_ref.shape
    column = lax.broadcasted_iota(jnp.int32, (half, quarter), 1) + pos[1] * quarter
    for k in range(mats):
        mine = jnp.where(column < settings[k, 0], p_ref[k].astype(F32), 0.0).astype(BF16)
        for zh in range(ZH):
            for zl in range(ZL):
                out_ref[zh, k, zl] = mine


def make_piece(pos, settings, projectors):
    mats, rows, rank_max = projectors.shape
    half, quarter = rows // ZL, rank_max // Y
    return pl.pallas_call(
        piece_kernel,
        out_shape=jax.ShapeDtypeStruct((ZH, mats, ZL, half, quarter), BF16),
        grid_spec=pltpu.PrefetchScalarGridSpec(
            num_scalar_prefetch=2,
            grid=(1,),
            in_specs=[
                pl.BlockSpec((mats, half, quarter), lambda i, pos, settings: (0, pos[0], pos[1]))
            ],
            out_specs=pl.BlockSpec(
                (ZH, mats, ZL, half, quarter), lambda i, pos, settings: (0, 0, 0, 0, 0)
            ),
        ),
        compiler_params=mib(4),
        name="piece",
    )(pos, settings, pltpu.with_memory_space_constraint(projectors, HBM))


def sides_kernel(pos, a_near, a_far, c_near, c_far, x_ref, xt_ref):
    tokens = a_near.shape[0]

    def write(projected, other):
        x_ref[:tokens, :] = projected[0]
        x_ref[tokens:, :] = projected[1]
        xt_ref[:, :tokens] = other[0].T
        xt_ref[:, tokens:] = other[1].T

    a = lambda: (a_near[...], a_far[...])
    c = lambda: (c_near[0], c_far[...])

    @pl.when(pos[1] == 0)
    def _():
        write(a(), c())

    @pl.when(pos[1] != 0)
    def _():
        write(c(), a())


def make_sides(pos, a_near, a_far, cotangents, c_far):
    tokens, features = a_near.shape
    chunk = 1024
    block = pl.BlockSpec((tokens, chunk), lambda j, pos: (0, j))
    return pl.pallas_call(
        sides_kernel,
        out_shape=(
            HBM((2 * tokens, features), BF16),
            HBM((features, 2 * tokens), BF16),
        ),
        grid_spec=pltpu.PrefetchScalarGridSpec(
            num_scalar_prefetch=1,
            grid=(features // chunk,),
            in_specs=[
                block,
                block,
                pl.BlockSpec((1, tokens, chunk), lambda j, pos: (pos[0], 0, j)),
                block,
            ],
            out_specs=(
                pl.BlockSpec((2 * tokens, chunk), lambda j, pos: (0, j)),
                pl.BlockSpec((chunk, 2 * tokens), lambda j, pos: (j, 0)),
            ),
        ),
        compiler_params=mib(20),
        name="sides",
    )(pos, *(pltpu.with_memory_space_constraint(v, HBM) for v in (a_near, a_far, cotangents, c_far)))


def update_kernel(
    scale, pos, settings, s_ref, m1_ref, m2_ref, near_ref, far_ref, w_ref,
    w_out, m1_out, m2_out, n_ref,
):
    mats = m1_ref.shape[0]
    half, quarter = s_ref.shape[3:]

    @pl.when(pl.program_id(0) == 0)
    def _():
        for k in range(mats):
            for y in range(Y):
                columns = slice(y * quarter, (y + 1) * quarter)
                column = lax.broadcasted_iota(jnp.int32, (half, quarter), 1) + y * quarter
                live = column < settings[k, 0]
                for z in range(ZL):
                    rows = slice(z * half, (z + 1) * half)
                    grad = s_ref[y, z, k].astype(F32) * scale
                    m1 = BETA_ONE * m1_ref[k, rows, columns] + (1.0 - BETA_ONE) * grad
                    m2 = BETA_TWO * m2_ref[k, rows, columns] + (1.0 - BETA_TWO) * grad * grad
                    m1 = jnp.where(live, m1, 0.0)
                    m2 = jnp.where(live, m2, 0.0)
                    m1_out[k, rows, columns] = m1
                    m2_out[k, rows, columns] = m2
                    normalized = jnp.where(live, m1 / (jnp.sqrt(m2) + EPSILON), 0.0)
                    n_ref[k, rows, columns] = normalized.astype(BF16)

    for k, p_ref in ((pos[0], near_ref), (1 - pos[0], far_ref)):
        rhs = p_ref[...].reshape(Y * quarter, p_ref.shape[2])
        update = jnp.dot(n_ref[k], rhs, preferred_element_type=F32)
        w_out[k] = (w_ref[k].astype(F32) - update).astype(BF16)


def apply_update(scale, pos, settings, s, m1, m2, near, far, weights):
    mats, rows, columns = weights.shape
    chunk = 2048

    def whole_block(shape):
        return pl.BlockSpec(shape, lambda j, *_: (0,) * len(shape))

    p_block = pl.BlockSpec((Y, near.shape[1], chunk), lambda j, *_: (0, 0, j))
    w_block = pl.BlockSpec((mats, rows, chunk), lambda j, *_: (0, 0, j))
    moments = whole_block(m1.shape)
    return pl.pallas_call(
        functools.partial(update_kernel, scale),
        out_shape=(
            jax.ShapeDtypeStruct(weights.shape, BF16),
            jax.ShapeDtypeStruct(m1.shape, F32),
            jax.ShapeDtypeStruct(m2.shape, F32),
        ),
        grid_spec=pltpu.PrefetchScalarGridSpec(
            num_scalar_prefetch=2,
            grid=(columns // chunk,),
            in_specs=[whole_block(s.shape), moments, moments, p_block, p_block, w_block],
            out_specs=(w_block, moments, moments),
            scratch_shapes=[pltpu.VMEM(m1.shape, BF16)],
        ),
        compiler_params=mib(24),
        name="update",
    )(pos, settings, s, m1, m2, near, far, weights)


def on_device(
    activations, cotangents, weights, projectors, first_moment, second_moment, matrix_settings
):
    mats, rows, rank_max = projectors.shape
    token_total = activations.shape[0] * 256
    grad_scale = 1.0 / math.sqrt(token_total)
    core = lax.axis_index("core")
    y = lax.axis_index("y")
    zl = lax.axis_index("zl")
    x = lax.axis_index("x")
    pos = jnp.stack([core, jnp.where(core == 0, x, y), jnp.where(core == 0, y, x)])
    pos = pos.astype(jnp.int32)
    live = jnp.arange(rank_max)[None, None, :] < matrix_settings[:, 0][:, None, None]
    half, quarter = rows // ZL, rank_max // Y

    far_index = 1 - core
    a_far = to_partner(activations)
    c_far = to_partner(lax.dynamic_index_in_dim(cotangents, far_index, 0, keepdims=False))

    piece = make_piece(jnp.stack([zl, y]).astype(jnp.int32), matrix_settings, projectors)
    g = swap_axes(piece.reshape(ZH * C * ZL, half, quarter), ("zh", "core", "zl"))
    g = g.reshape(ZH, 256, quarter)
    narrow, wide = {}, {}
    for o in (1, 3, 2):
        narrow[o] = shift(g, NARROW, o)
    for o in (1, 3, 2):
        wide[o] = shift(g, WIDE, o)
    rest = jnp.stack(
        [narrow[o].reshape(2, ZH // 2, 256, quarter) for o in (1, 3, 2)], axis=1
    )
    ahead = shift(rest, WIDE, 1)
    behind = shift(rest, WIDE, 3)
    low = shift(ahead[0], WIDE, 1)
    high = shift(behind[1], WIDE, 3)

    others = (-1, -3, -2)
    blocks_a = [(g[None], 0, (0,), 0)]
    blocks_a += [(narrow[o][None], 0, (-o,), 0) for o in (1, 3, 2)]
    blocks_a += [(wide[o][None], -o, (0,), 0) for o in (1, 3, 2)]
    blocks_b = [(ahead, -1, others, 0), (behind, -3, others, 0)]
    blocks_c = [(low, -2, others, 0), (high, -2, others, ZH // 2)]

    side = lax.dynamic_index_in_dim(matrix_settings[:, 1], core, 0, keepdims=False)
    projected_side, other_side = make_sides(
        jnp.stack([core, side]).astype(jnp.int32), activations, a_far, cotangents, c_far
    )
    other_side = other_side.reshape(ZH, X, 256, 512)

    acc = coeffs_step(pos, projected_side, blocks_a)
    acc = coeffs_step(pos, projected_side, blocks_b, acc)
    coeffs = coeffs_step(pos, projected_side, blocks_c, acc, last=True)

    away = (1, 2, 3)
    parts = []
    for o in (2, 1, 3):
        (block,) = grad_blocks(pos, other_side, coeffs, (o, away))
        parts.append(shift(block, WIDE, o))
    own_away, *home = grad_blocks(
        pos, other_side, coeffs, (0, away), *((o, (0,)) for o in (2, 1, 3, 0))
    )
    full = in_order(pos, blocks_a + blocks_b + blocks_c)
    full_far = to_partner(full)
    s = own_away.astype(F32)
    for part in parts:
        s = s + part.astype(F32)
    s = s.astype(BF16)
    total = home[3].astype(F32)
    narrows = []
    for i, o in enumerate(away):
        narrows.append(shift(s[i], NARROW, o))
    for i, o in enumerate((2, 1, 3)):
        total = total + shift(home[i], WIDE, o).astype(F32)
    for part in narrows:
        total = total + part.astype(F32)
    s = total.astype(BF16)
    s = swap_axes(s.reshape(ZH * C * ZL, half, quarter), ("zh", "core", "zl"))
    s = s.astype(F32).reshape(ZH, mats, ZL, half, quarter)
    s = jnp.sum(s, axis=(0, 2)).astype(BF16)
    s = swap_axes(repeat(s, Y * ZL), ("y", "zl"))
    return apply_update(
        grad_scale,
        pos,
        matrix_settings,
        s.reshape(Y, ZL, mats, half, quarter),
        first_moment,
        second_moment,
        full,
        full_far,
        weights,
    )


def solution(mesh):
    split = Mesh(mesh.devices.reshape(SIZES), NAMES)
    owner = ("zh", "x", "core")
    return jax.shard_map(
        on_device,
        mesh=split,
        in_specs=(
            P(NAMES, None),
            P(None, NAMES, None),
            P(None, owner, None),
            P(None, owner, None),
            P(None, owner, None),
            P(None, owner, None),
            P(),
        ),
        out_specs=(P(None, owner, None), P(None, owner, None), P(None, owner, None)),
        check_vma=False,
    )
```

```python
import functools
import math

import jax
import jax.numpy as jnp
from jax import lax
from jax.experimental import pallas as pl
from jax.experimental.pallas import tpu as pltpu
from jax.sharding import Mesh, PartitionSpec as P


BETA_ONE = 0.9
BETA_TWO = 0.95
EPSILON = 1e-08
ZH, X, C, Y, ZL = SIZES = (4, 4, 2, 4, 2)
NAMES = ("zh", "x", "core", "y", "zl")
BF16 = jnp.bfloat16
F32 = jnp.float32
VMEM = pltpu.MemorySpace.VMEM
SMEM = pltpu.MemorySpace.SMEM
HBM = pltpu.MemorySpace.HBM


def mib(count):
    return pltpu.CompilerParams(vmem_limit_bytes=count << 20)


def flat_index(zh, x, c, y, zl):
    return (((zh * X + x) * C + c) * Y + y) * ZL + zl


def line_groups(axis_of_core):
    groups = []
    for c in range(C):
        for zh in range(ZH):
            for zl in range(ZL):
                for fixed in range(4):
                    if axis_of_core[c] == "x":
                        groups.append([flat_index(zh, i, c, fixed, zl) for i in range(X)])
                    else:
                        groups.append([flat_index(zh, fixed, c, i, zl) for i in range(Y)])
    return groups


WIDE = line_groups("xy")
NARROW = line_groups("yx")


def shift(v, groups, offset):
    pairs = [(g[i], g[(i + offset) % 4]) for g in groups for i in range(4)]
    return lax.ppermute(v, NAMES, pairs)


def swap_axes(v, axes):
    return lax.all_to_all(v, axes, split_axis=0, concat_axis=0, tiled=True)


def repeat(v, n):
    return jnp.broadcast_to(v[None], (n,) + v.shape)


def to_partner(v):
    return lax.ppermute(v, "core", [(0, 1), (1, 0)])


def place(core, a, b):
    first = core == 0
    return jnp.where(first, a, b), jnp.where(first, b, a)


def offset(position, shift_by):
    return (position + shift_by) & 3


def views(block, zh_from):
    if len(block.shape) == 4:
        return [(block, zh_from)]
    return [(block.at[h], zh_from + h * block.shape[2]) for h in range(block.shape[0])]


def coeffs_kernel(items, first, last, pos, x_ref, *refs):
    blocks, refs = refs[: len(items)], refs[len(items) :]
    acc = refs[-1]
    if first:
        acc[...] = jnp.zeros_like(acc)
    else:
        acc[...] = refs[0][...]
    for (a_off, b_offs, start), whole_block in zip(items, blocks):
        for i, b_off, (block, zh_from) in [
            (i, b_off, view)
            for view in views(whole_block, start)
            for i, b_off in enumerate(b_offs)
        ]:
            count = block.shape[1]
            x, y = place(pos[0], offset(pos[1], a_off), offset(pos[2], b_off))
            lhs = jnp.concatenate(
                [
                    x_ref[:, pl.ds(pl.multiple_of((zh * X + x) * 256, 256), 256)]
                    for zh in range(zh_from, zh_from + count)
                ],
                axis=1,
            )
            rhs = block[i].reshape(count * 256, 128)
            acc[y] += jnp.dot(lhs, rhs, preferred_element_type=F32)
    if last:
        refs[-2][...] = acc[...].astype(BF16)


def coeffs_step(pos, x, blocks, acc=None, last=False):
    shape = (4, x.shape[0], 128)
    items = tuple(block[1:] for block in blocks)
    ins = [pos, x, *(block[0] for block in blocks)] + ([] if acc is None else [acc])
    return pl.pallas_call(
        functools.partial(coeffs_kernel, items, acc is None, last),
        out_shape=jax.ShapeDtypeStruct(shape, BF16 if last else F32),
        in_specs=[pl.BlockSpec(memory_space=SMEM)]
        + [pl.BlockSpec(memory_space=VMEM)] * (len(ins) - 1),
        out_specs=pl.BlockSpec(memory_space=VMEM),
        scratch_shapes=[pltpu.VMEM(shape, F32)] if last else [],
        compiler_params=mib(14),
        name="coeffs",
    )(*ins)


def grad_kernel(items, pos, xt_ref, coeffs_ref, *out_refs):
    for (a_off, b_offs), out_ref in zip(items, out_refs):
        for i, b_off in enumerate(b_offs):
            x, y = place(pos[0], offset(pos[1], a_off), offset(pos[2], b_off))
            lhs = jnp.concatenate([xt_ref[zh, x] for zh in range(ZH)], axis=0)
            part = jnp.dot(lhs, coeffs_ref[y], preferred_element_type=F32)
            out_ref[i] = part.astype(BF16).reshape(ZH, 256, 128)


def grad_blocks(pos, xt, coeffs, *items):
    shapes = [
        jax.ShapeDtypeStruct((len(b_offs), ZH, 256, 128), BF16) for _, b_offs in items
    ]
    return pl.pallas_call(
        functools.partial(grad_kernel, items),
        out_shape=shapes,
        in_specs=[pl.BlockSpec(memory_space=SMEM)] + [pl.BlockSpec(memory_space=VMEM)] * 2,
        out_specs=[pl.BlockSpec(memory_space=VMEM)] * len(shapes),
        compiler_params=mib(12),
        name="grads",
    )(pos, xt, coeffs)


def order_kernel(items, pos, *refs):
    out_ref = refs[-1]
    for (a_off, b_offs, start), whole_block in zip(items, refs):
        for i, b_off, (block, zh_from) in [
            (i, b_off, view)
            for view in views(whole_block, start)
            for i, b_off in enumerate(b_offs)
        ]:
            x, y = place(pos[0], offset(pos[1], a_off), offset(pos[2], b_off))
            for j in range(block.shape[1]):
                lanes = pl.ds(pl.multiple_of(((zh_from + j) * X + x) * 256, 256), 256)
                out_ref[y, :, lanes] = block[i, j].T


def in_order(pos, blocks):
    return pl.pallas_call(
        functools.partial(order_kernel, tuple(block[1:] for block in blocks)),
        out_shape=jax.ShapeDtypeStruct((Y, 128, ZH * X * 256), BF16),
        in_specs=[pl.BlockSpec(memory_space=SMEM)]
        + [pl.BlockSpec(memory_space=VMEM)] * len(blocks),
        out_specs=pl.BlockSpec(memory_space=VMEM),
        compiler_params=mib(12),
        name="order",
    )(pos, *(block[0] for block in blocks))


def piece_kernel(pos, settings, p_ref, out_ref):
    mats, half, quarter = p_ref.shape
    column = lax.broadcasted_iota(jnp.int32, (half, quarter), 1) + pos[4] * quarter
    for k in range(mats):
        mine = jnp.where(column < settings[k, 0], p_ref[k].astype(F32), 0.0).astype(BF16)
        for zh in range(ZH):
            for zl in range(ZL):
                out_ref[zh, k, zl] = mine


def make_piece(pos, settings, projectors):
    mats, rows, rank_max = projectors.shape
    half, quarter = rows // ZL, rank_max // Y
    return pl.pallas_call(
        piece_kernel,
        out_shape=jax.ShapeDtypeStruct((ZH, mats, ZL, half, quarter), BF16),
        grid_spec=pltpu.PrefetchScalarGridSpec(
            num_scalar_prefetch=2,
            grid=(1,),
            in_specs=[
                pl.BlockSpec((mats, half, quarter), lambda i, pos, settings: (0, pos[3], pos[4]))
            ],
            out_specs=pl.BlockSpec(
                (ZH, mats, ZL, half, quarter), lambda i, pos, settings: (0, 0, 0, 0, 0)
            ),
        ),
        compiler_params=mib(4),
        name="piece",
    )(pos, settings, pltpu.with_memory_space_constraint(projectors, HBM))


def sides_kernel(pos, settings, a_near, a_far, c_near, c_far, x_ref, xt_ref):
    tokens = a_near.shape[0]

    def write(projected, other):
        x_ref[:tokens, :] = projected[0]
        x_ref[tokens:, :] = projected[1]
        xt_ref[:, :tokens] = other[0].T
        xt_ref[:, tokens:] = other[1].T

    a = lambda: (a_near[...], a_far[...])
    c = lambda: (c_near[0], c_far[0])

    @pl.when(settings[pos[0], 1] == 0)
    def _():
        write(a(), c())

    @pl.when(settings[pos[0], 1] != 0)
    def _():
        write(c(), a())


def make_sides(pos, settings, a_near, a_far, cotangents, c_far):
    tokens, features = a_near.shape
    chunk = 1024
    block = pl.BlockSpec((tokens, chunk), lambda j, pos, settings: (0, j))
    return pl.pallas_call(
        sides_kernel,
        out_shape=(
            HBM((2 * tokens, features), BF16),
            HBM((features, 2 * tokens), BF16),
        ),
        grid_spec=pltpu.PrefetchScalarGridSpec(
            num_scalar_prefetch=2,
            grid=(features // chunk,),
            in_specs=[
                block,
                block,
                pl.BlockSpec((1, tokens, chunk), lambda j, pos, settings: (pos[0], 0, j)),
                pl.BlockSpec((1, tokens, chunk), lambda j, pos, settings: (pos[0], 0, j)),
            ],
            out_specs=(
                pl.BlockSpec((2 * tokens, chunk), lambda j, pos, settings: (0, j)),
                pl.BlockSpec((chunk, 2 * tokens), lambda j, pos, settings: (j, 0)),
            ),
        ),
        compiler_params=mib(20),
        name="sides",
    )(
        pos,
        settings,
        pltpu.with_memory_space_constraint(a_near, HBM),
        a_far,
        pltpu.with_memory_space_constraint(cotangents, HBM),
        c_far,
    )


def update_kernel(
    scale, pos, settings, s_ref, m1_ref, m2_ref, near_ref, far_ref, w_ref,
    w_out, m1_out, m2_out, n_ref,
):
    mats = m1_ref.shape[0]
    half, quarter = s_ref.shape[3:]

    @pl.when(pl.program_id(0) == 0)
    def _():
        for k in range(mats):
            for y in range(Y):
                columns = slice(y * quarter, (y + 1) * quarter)
                column = lax.broadcasted_iota(jnp.int32, (half, quarter), 1) + y * quarter
                live = column < settings[k, 0]
                for z in range(ZL):
                    rows = slice(z * half, (z + 1) * half)
                    grad = s_ref[y, z, k].astype(F32) * scale
                    m1 = BETA_ONE * m1_ref[k, rows, columns] + (1.0 - BETA_ONE) * grad
                    m2 = BETA_TWO * m2_ref[k, rows, columns] + (1.0 - BETA_TWO) * grad * grad
                    m1 = jnp.where(live, m1, 0.0)
                    m2 = jnp.where(live, m2, 0.0)
                    m1_out[k, rows, columns] = m1
                    m2_out[k, rows, columns] = m2
                    normalized = jnp.where(live, m1 / (jnp.sqrt(m2) + EPSILON), 0.0)
                    n_ref[k, rows, columns] = normalized.astype(BF16)

    for k, p_ref in ((pos[0], near_ref), (1 - pos[0], far_ref)):
        rhs = p_ref[...].reshape(Y * quarter, p_ref.shape[2])
        update = jnp.dot(n_ref[k], rhs, preferred_element_type=F32)
        w_out[k] = (w_ref[k].astype(F32) - update).astype(BF16)


def apply_update(scale, pos, settings, s, m1, m2, near, far, weights):
    mats, rows, columns = weights.shape
    chunk = columns

    def whole_block(shape):
        return pl.BlockSpec(shape, lambda j, *_: (0,) * len(shape))

    p_block = pl.BlockSpec((Y, near.shape[1], chunk), lambda j, *_: (0, 0, j))
    w_block = pl.BlockSpec((mats, rows, chunk), lambda j, *_: (0, 0, j))
    moments = whole_block(m1.shape)
    return pl.pallas_call(
        functools.partial(update_kernel, scale),
        out_shape=(
            jax.ShapeDtypeStruct(weights.shape, BF16),
            jax.ShapeDtypeStruct(m1.shape, F32),
            jax.ShapeDtypeStruct(m2.shape, F32),
        ),
        grid_spec=pltpu.PrefetchScalarGridSpec(
            num_scalar_prefetch=2,
            grid=(columns // chunk,),
            in_specs=[whole_block(s.shape), moments, moments, p_block, p_block, w_block],
            out_specs=(w_block, moments, moments),
            scratch_shapes=[pltpu.VMEM(m1.shape, BF16)],
        ),
        compiler_params=mib(40),
        name="update",
    )(
        pos,
        settings,
        s,
        m1,
        m2,
        near,
        far,
        pltpu.with_memory_space_constraint(weights, HBM),
    )


def on_device(
    activations, cotangents, weights, projectors, first_moment, second_moment, matrix_settings
):
    mats, rows, rank_max = projectors.shape
    token_total = activations.shape[0] * 256
    grad_scale = 1.0 / math.sqrt(token_total)
    core = lax.axis_index("core")
    y = lax.axis_index("y")
    zl = lax.axis_index("zl")
    x = lax.axis_index("x")
    pos = jnp.stack([core, jnp.where(core == 0, x, y), jnp.where(core == 0, y, x), zl, y])
    pos = pos.astype(jnp.int32)
    live = jnp.arange(rank_max)[None, None, :] < matrix_settings[:, 0][:, None, None]
    half, quarter = rows // ZL, rank_max // Y

    a_far = to_partner(activations)
    c_far = to_partner(cotangents)

    piece = make_piece(pos, matrix_settings, projectors)
    g = swap_axes(piece.reshape(ZH * C * ZL, half, quarter), ("zh", "core", "zl"))
    g = g.reshape(ZH, 256, quarter)
    narrow, wide = {}, {}
    for o in (1, 3, 2):
        narrow[o] = shift(g, NARROW, o)
    for o in (1, 3, 2):
        wide[o] = shift(g, WIDE, o)
    low, high = (
        jnp.stack([narrow[o][part] for o in (1, 3, 2)])
        for part in (slice(0, ZH // 2), slice(ZH // 2, ZH))
    )
    lows, highs = {}, {}
    lows[1] = shift(low, WIDE, 1)
    highs[3] = shift(high, WIDE, 3)
    highs[1] = shift(high, WIDE, 1)
    lows[3] = shift(low, WIDE, 3)
    lows[2] = shift(lows[1], WIDE, 1)
    highs[2] = shift(highs[3], WIDE, 3)

    others = (-1, -3, -2)
    blocks_a = [(g[None], 0, (0,), 0)]
    blocks_a += [(narrow[o][None], 0, (-o,), 0) for o in (1, 3, 2)]
    blocks_a += [(wide[o][None], -o, (0,), 0) for o in (1, 3, 2)]
    blocks_b, blocks_c = (
        [
            block
            for o in offsets
            for block in ((lows[o], -o, others, 0), (highs[o], -o, others, ZH // 2))
        ]
        for offsets in ((1, 3), (2,))
    )

    projected_side, other_side = make_sides(
        pos, matrix_settings, activations, a_far, cotangents, c_far
    )
    other_side = other_side.reshape(ZH, X, 256, 512)

    acc = coeffs_step(pos, projected_side, blocks_a)
    acc = coeffs_step(pos, projected_side, blocks_b, acc)
    coeffs = coeffs_step(pos, projected_side, blocks_c, acc, last=True)

    away = (1, 2, 3)
    parts = []
    for o in (2, 1, 3):
        (block,) = grad_blocks(pos, other_side, coeffs, (o, away))
        parts.append(shift(block, WIDE, o))
    own_away, *home = grad_blocks(
        pos, other_side, coeffs, (0, away), *((o, (0,)) for o in (2, 1, 3, 0))
    )
    full = in_order(pos, blocks_a + blocks_b + blocks_c)
    full_far = to_partner(full)
    s = own_away.astype(F32)
    for part in parts:
        s = s + part.astype(F32)
    s = s.astype(BF16)
    total = home[3].astype(F32)
    narrows = []
    for i, o in enumerate(away):
        narrows.append(shift(s[i], NARROW, o))
    for i, o in enumerate((2, 1, 3)):
        total = total + shift(home[i], WIDE, o).astype(F32)
    for part in narrows:
        total = total + part.astype(F32)
    s = total.astype(BF16)
    s = swap_axes(s.reshape(ZH * C * ZL, half, quarter), ("zh", "core", "zl"))
    s = s.astype(F32).reshape(ZH, mats, ZL, half, quarter)
    s = jnp.sum(s, axis=(0, 2)).astype(BF16)
    s = swap_axes(repeat(s, Y * ZL), ("y", "zl"))
    return apply_update(
        grad_scale,
        pos,
        matrix_settings,
        s.reshape(Y, ZL, mats, half, quarter),
        first_moment,
        second_moment,
        full,
        full_far,
        weights,
    )


def solution(mesh):
    split = Mesh(mesh.devices.reshape(SIZES), NAMES)
    owner = ("zh", "x", "core")
    return jax.shard_map(
        on_device,
        mesh=split,
        in_specs=(
            P(NAMES, None),
            P(None, NAMES, None),
            P(None, owner, None),
            P(None, owner, None),
            P(None, owner, None),
            P(None, owner, None),
            P(),
        ),
        out_specs=(P(None, owner, None), P(None, owner, None), P(None, owner, None)),
        check_vma=False,
    )
```
